32 devices in a mesh: facet: 4 (over z), strip: 8 (over y, x, core).
Axes of the slice: x: 2, y: 2, z: 4, core: 2. Of those that a mesh axis runs over, the one named last changes fastest.
Arguments:
- sky_components: bfloat16 [4, 2, 4, 2048, 2048], P('facet', None, None, 'strip'), may hold values from -6 to 6
- scale_kernels: float32 [4, 33], replicated, may hold values from 0.026111647 to 0.26111647
- row_taper: bfloat16 [4, 2048, 512], P('facet'), may hold values from -0.125 to 0.125
- col_taper: bfloat16 [4, 2048, 1024], P('facet'), may hold values from -0.125 to 0.125
- finish_rows: bfloat16 [4, 512, 128], replicated, may hold values from -0.25 to 0.25
- finish_cols: bfloat16 [4, 512, 128], replicated, may hold values from -0.5 to 0.5
- subgrid_owner: int32 [32], replicated, may hold values from 0 to 31, as said below
- block_cell: int32 [2048, 2], P(('facet', 'strip')), may hold values from 0 to 480
- vis_offset: float32 [2048, 2, 128], P(('facet', 'strip')), may hold values from 0 to 31
- block_owner: int32 [2048, 1], P(('facet', 'strip')), may hold values from 0 to 31; in each aligned block of 64 rows (0 to 63, 64 to 127, ...) at most 4 rows name the same one
- observed: float32 [4096, 2, 128], P(('facet', 'strip')), may hold values from -6 to 6
- antenna_pair_index: int32 [4096, 2, 128], P(('facet', 'strip')), may hold values from 0 to 511
- gains: float32 [2, 512], replicated, may hold values from 0.1 to 1.9
Outputs:
- subgrids: bfloat16 [32, 2, 512, 512], P(('facet', 'strip'))
- residual: float32 [4096, 2, 128], P(('facet', 'strip'))
The draws below stay inside these ranges and needn't reach their ends.
Inputs may be any that keep to these rules, and one draw needn't show every extreme that they name: Every device number appears once; subgrid_owner[a * 8 + b] = rowperm(a) * 8 + colperm(b) for a permutation rowperm of the subgrid rows and a permutation colperm of the subgrid columns. `block_owner`: among the 64 blocks of one device at most 4 share an owner, and some owner takes exactly 4 of them.
All inputs are finite; a program needn't handle non-finite values.
Results may differ from the reference program's by a relative error of at most 0.02.
Values may be sent and summed in bfloat16 or wider, within the bound.
A program may use at most 128 MiB of HBM per device.

```python
import math
import jax
import jax.numpy as jnp
import numpy as np
from jax import lax

FS = 2048
CM = 128
SG = 512
TILE = 32
BLOCK_VISIBILITY = 128
CORRELATION_NUM = 2
SCALES = 4
HALF = 16
ANTENNA_COUNT = 512
BLK = 64
FACETS = 4
SUBROWS = 4
SUBCOLS = 8
SUBGRID_COUNT = 32
RECEIVE_BLOCKS = 4


def draw_subgrid_owner(key, part):
    row_perm = jax.random.permutation(jax.random.fold_in(key, 11), SUBROWS).astype(jnp.int32)
    col_perm = jax.random.permutation(jax.random.fold_in(key, 23), SUBCOLS).astype(jnp.int32)
    grid_ids = jnp.arange(SUBGRID_COUNT, dtype=jnp.int32)
    return (row_perm[grid_ids // SUBCOLS] * SUBCOLS + col_perm[grid_ids % SUBCOLS]).astype(jnp.int32)


def plant(array, own_key, low, largest):
    index_at = [jax.random.randint(jax.random.fold_in(own_key, axis), (), 0, length) for axis, length in enumerate(array.shape)]
    main_axis = array.shape.index(max(array.shape))
    neighbour = index_at[:main_axis] + [(index_at[main_axis] + 1) % array.shape[main_axis]] + index_at[main_axis + 1:]
    return array.at[tuple(index_at)].set(low).at[tuple(neighbour)].set(largest)


def block_scale(key, dims, split, smallest, top_value):
    level, own = 1.0, jax.random.fold_in(key, 6)
    for axis_at, shards_of in split:
        draws = jnp.exp(jax.random.uniform(jax.random.fold_in(own, axis_at), (shards_of,), jnp.float32, smallest / len(split), top_value / len(split)))
        level = level * jnp.repeat(draws, dims[axis_at] // shards_of).reshape([-1 if axis == axis_at else 1 for axis in range(len(dims))])
    return level


def shared_out(rng, own, number, rows, count, top, bound, skew):
    sequence = jax.random.permutation(rng, count)
    crowded, ordinary = shares(count, rows * top, bound, skew, True), shares(count, rows * top, bound, skew, False)
    places = jnp.arange(count)

    def named(tallies, offset_by):
        used = int((tallies > 0).sum())
        fixed = max(1, used // 4)
        passed = fixed + (places - fixed + offset_by * (used - fixed)) % max(1, count - fixed)
        return jnp.zeros((count,), jnp.int32).at[sequence[jnp.where(places < fixed, places, passed)]].set(jnp.asarray(tallies, jnp.int32))

    tallies = jnp.where(number % 4 == 0, named(crowded, number // 4), named(ordinary, number - number // 4 - 1))
    mixed = jax.random.permutation(jax.random.fold_in(own, 3), count)
    giver, taker = mixed[0:count // 2 * 2:2], mixed[1:count // 2 * 2:2]
    slack = jnp.minimum(tallies[giver] - 1, bound - tallies[taker]) // 2
    slack = jnp.where((giver == sequence[0]) | (taker == sequence[0]) | (tallies[taker] == 0), 0, jnp.maximum(slack, 0))
    passed = jax.random.randint(jax.random.fold_in(own, 4), (count // 2,), 0, 1 << 20) % (slack + 1)
    tallies = tallies.at[giver].add(-passed).at[taker].add(passed)
    labels = jnp.searchsorted(jnp.cumsum(tallies), jnp.arange(rows * top), side="right").astype(jnp.int32)
    listing = labels.reshape(top, rows).T
    listing = listing[jax.random.permutation(jax.random.fold_in(own, 1), rows)]
    offset_by = jax.random.randint(jax.random.fold_in(own, 2), (rows, 1), 0, top)
    return jnp.take_along_axis(listing, (jnp.arange(top)[None, :] + offset_by) % top, axis=1)


def shares(number_of, total, limit, lean, full):
    weights = [(1 << 20) // math.isqrt(grade ** lean) + 1 for grade in range(1, number_of + 1)]
    largest = limit if full else min(limit, max(-(-total // number_of), total * weights[0] // sum(weights)))
    least = 1 if total - largest >= number_of - 1 else 0
    holding, surplus = [largest] + [least] * (number_of - 1), total - largest - least * (number_of - 1)
    while surplus > 0:
        candidates = [i for i in range(1, number_of) if holding[i] < largest] or [i for i in range(1, number_of) if holding[i] < limit]
        pool, left = sum([weights[i] for i in candidates]), surplus
        for i in candidates:
            extra = min(limit - holding[i], max(1, left * weights[i] // pool), surplus)
            holding[i] = holding[i] + extra
            surplus = surplus - extra
    return np.array(holding)


def gaussian(rng, shape, deviation, most, pieces=(), kind=jnp.bfloat16):
    values = jax.random.normal(rng, shape, jnp.float32) * deviation
    if len(pieces) > 0:
        values = block_scale(rng, shape, pieces, -0.22, 0.18) * values
    return jnp.clip(values, min=-most, max=most).astype(kind)


def setup_inputs(seed: int = 0) -> dict:
    arg_keys = jax.random.split(jax.random.key(seed), 14)
    sky_components = gaussian(arg_keys[0], (FACETS, CORRELATION_NUM, SCALES, FS, FS), 1.0, 6.0, ((0, 4), (3, 8)))
    scale_kernels = jnp.clip(jnp.exp(jax.random.uniform(arg_keys[1], (SCALES, 2 * HALF + 1), jnp.float32, math.log(0.026111647), math.log(0.26111647))), 0.026111647, 0.26111647)
    row_taper = gaussian(arg_keys[2], (FACETS, FS, SUBROWS * CM), FS ** -0.5, 0.125, ((0, 4),))
    col_taper = gaussian(arg_keys[3], (FACETS, FS, SUBCOLS * CM), FS ** -0.5, 0.125, ((0, 4),))
    finish_rows = gaussian(arg_keys[4], (FACETS, SG, CM), (FACETS * CM) ** -0.5, 0.25)
    finish_cols = gaussian(arg_keys[5], (FACETS, SG, CM), CM ** -0.5, 0.5)
    subgrid_owner = draw_subgrid_owner(jax.random.fold_in(arg_keys[13], 71), 0)
    block_cell = plant(jax.random.randint(arg_keys[7], (SUBGRID_COUNT * BLK, 2), 0, SG - TILE + 1), jax.random.fold_in(arg_keys[7], 1), 0, SG - TILE).astype(jnp.int32)
    vis_offset = jnp.clip(31.0 * jax.random.uniform(arg_keys[8], (SUBGRID_COUNT * BLK, 2, BLOCK_VISIBILITY), jnp.float32) ** block_scale(arg_keys[8], (SUBGRID_COUNT * BLK, 2, BLOCK_VISIBILITY), ((0, 32),), -0.2, 0.2), 0.0, 31.0)
    block_owner_keys = jax.random.split(jax.random.fold_in(arg_keys[9], 1), (SUBGRID_COUNT * BLK) // BLK)
    block_owner_turns = jax.random.permutation(jax.random.fold_in(arg_keys[9], 3), (SUBGRID_COUNT * BLK) // BLK)
    block_owner = jax.vmap(lambda own, number: shared_out(jax.random.fold_in(arg_keys[9], 2), own, number, BLK, SUBGRID_COUNT, 1, RECEIVE_BLOCKS, 2))(block_owner_keys, block_owner_turns).reshape((SUBGRID_COUNT * BLK, 1))
    observed = gaussian(arg_keys[10], (SUBGRID_COUNT * SUBGRID_COUNT * RECEIVE_BLOCKS, CORRELATION_NUM, BLOCK_VISIBILITY), 1.0, 6.0, ((0, 32),), jnp.float32)
    antenna_pair_index = plant(jax.random.randint(arg_keys[11], (SUBGRID_COUNT * SUBGRID_COUNT * RECEIVE_BLOCKS, 2, BLOCK_VISIBILITY), 0, ANTENNA_COUNT), jax.random.fold_in(arg_keys[11], 1), 0, ANTENNA_COUNT - 1).astype(jnp.int32)
    gains = jnp.clip(1.0 + 0.18 * jax.random.normal(arg_keys[12], (CORRELATION_NUM, ANTENNA_COUNT), jnp.float32), 0.1, 1.9)
    return dict(sky_components=sky_components, scale_kernels=scale_kernels, row_taper=row_taper, col_taper=col_taper, finish_rows=finish_rows, finish_cols=finish_cols, subgrid_owner=subgrid_owner, block_cell=block_cell, vis_offset=vis_offset, block_owner=block_owner, observed=observed, antenna_pair_index=antenna_pair_index, gains=gains)


KERNEL_WIDTH = 1.5


def smooth_rows_cols(padded, kernels, rows):
    taps = kernels.shape[1]
    width = (taps - 1) // 2
    along_rows = jnp.zeros(padded.shape[:2] + (rows, padded.shape[3]), jnp.float32)
    for tap in range(taps):
        along_rows = along_rows + kernels[:, tap][None, :, None, None] * padded[:, :, tap:tap + rows, :].astype(jnp.float32)
    cols = along_rows.shape[3]
    wide = jnp.pad(along_rows, ((0, 0), (0, 0), (0, 0), (width, width)))
    total = jnp.zeros_like(along_rows)
    for tap in range(taps):
        total = total + kernels[:, tap][None, :, None, None] * wide[:, :, :, tap:tap + cols]
    return jnp.sum(total, axis=1).astype(jnp.bfloat16)


def weights_of(offset):
    places = jnp.arange(TILE).astype(jnp.float32)
    delta = (places[None, None, :] - offset[:, :, None]) / KERNEL_WIDTH
    return jnp.exp(-0.5 * delta * delta)


def reference(sky_components, scale_kernels, row_taper, col_taper, finish_rows, finish_cols, subgrid_owner, block_cell, vis_offset, block_owner, observed, antenna_pair_index, gains):
    width = HALF

    def one_facet(index):
        comp = sky_components[index]
        padded = jnp.pad(comp, ((0, 0), (0, 0), (width, width), (0, 0)))
        smoothed = smooth_rows_cols(padded, scale_kernels, FS)
        col_products = jnp.einsum('crw,wk->crk', smoothed.astype(jnp.float32), col_taper[index].astype(jnp.float32)).astype(jnp.bfloat16)
        col_products = col_products.reshape(CORRELATION_NUM, FS, SUBCOLS, CM)
        rows_t = row_taper[index].reshape(FS, SUBROWS, CM)
        return jnp.einsum('rai,crbj->cabij', rows_t.astype(jnp.float32), col_products.astype(jnp.float32)).astype(jnp.bfloat16)

    contributions = lax.map(one_facet, jnp.arange(FACETS, dtype=jnp.int32))
    numbers = jnp.arange(SUBGRID_COUNT, dtype=jnp.int32)
    home = jnp.sum(jnp.where(subgrid_owner[None, :] == numbers[:, None], numbers[None, :], 0), axis=1).astype(jnp.int32)

    def one_device(device):
        grid_id = home[device]
        row_id = grid_id // SUBCOLS
        col_id = grid_id % SUBCOLS
        mine = contributions[:, :, row_id, col_id]
        spread = jnp.einsum('fcij,fsj->fcis', mine.astype(jnp.float32), finish_cols.astype(jnp.float32)).astype(jnp.bfloat16)
        subgrid = jnp.einsum('fri,fcis->crs', finish_rows.astype(jnp.float32), spread.astype(jnp.float32)).astype(jnp.bfloat16)
        cells = lax.dynamic_slice_in_dim(block_cell, device * BLK, BLK, 0)
        offsets = lax.dynamic_slice_in_dim(vis_offset, device * BLK, BLK, 0)

        def cut_tile(corner):
            return lax.dynamic_slice(subgrid, (jnp.int32(0), corner[0], corner[1]), (CORRELATION_NUM, TILE, TILE))

        tiles = jax.vmap(cut_tile)(cells)
        row_weights = weights_of(offsets[:, 0, :]).astype(jnp.bfloat16)
        col_weights = weights_of(offsets[:, 1, :])
        partial_value = jnp.einsum('kvi,kcij->kcvj', row_weights.astype(jnp.float32), tiles.astype(jnp.float32))
        predicted = jnp.sum(partial_value * col_weights[:, None, :, :], axis=3)
        return subgrid, predicted

    subgrids, predicted = lax.map(one_device, numbers)
    dest = block_owner[:, 0].reshape(SUBGRID_COUNT, BLK)
    same = dest[:, :, None] == dest[:, None, :]
    order = jnp.arange(BLK, dtype=jnp.int32)
    earlier = order[None, :] < order[:, None]
    rank = jnp.sum((same & earlier[None, :, :]).astype(jnp.int32), axis=2)
    slot = dest * (SUBGRID_COUNT * RECEIVE_BLOCKS) + numbers[:, None] * RECEIVE_BLOCKS + rank
    placed = jnp.zeros(observed.shape, jnp.float32).at[slot.reshape(-1)].set(predicted.reshape(SUBGRID_COUNT * BLK, CORRELATION_NUM, BLOCK_VISIBILITY))
    gain_p = jnp.take(gains, antenna_pair_index[:, 0, :], axis=1)
    gain_q = jnp.take(gains, antenna_pair_index[:, 1, :], axis=1)
    product = jnp.transpose(gain_p * gain_q, (1, 0, 2))
    residual = observed - product * placed
    return subgrids, residual
```

```python
import jax
import jax.numpy as jnp
from jax import lax
from jax.experimental import pallas as pl
from jax.experimental.pallas import tpu as pltpu
from jax.sharding import PartitionSpec as P

TILE = 32


KERNEL_WIDTH = 1.5


LANES = 128
COL_TILE = 256


def halo_rows(x, axis, dim, width):
    count, length = (lax.axis_size(axis), x.shape[dim])
    up = [(i, (i + 1) % count) for i in range(count - 1)]
    down = [(j, i) for i, j in up]
    last = lax.slice_in_dim(x, length - width, length, axis=dim)
    initial = lax.slice_in_dim(x, 0, width, axis=dim)
    return lax.ppermute(last, axis, up), lax.ppermute(initial, axis, down)


def band_matrices(kernels):
    taps = kernels.shape[1]
    width = (taps - 1) // 2
    span = LANES + taps - 1
    k = lax.broadcasted_iota(jnp.int32, (span, LANES), 0)
    n = lax.broadcasted_iota(jnp.int32, (span, LANES), 1)
    i = lax.broadcasted_iota(jnp.int32, (LANES, span), 0)
    m = lax.broadcasted_iota(jnp.int32, (LANES, span), 1)
    down = jnp.zeros((kernels.shape[0], span, LANES), jnp.float32)
    across = jnp.zeros((kernels.shape[0], LANES, span), jnp.float32)
    for t in range(taps):
        tap = kernels[:, t][:, None, None]
        down = jnp.where((k - n == t)[None], tap, down)
        across = jnp.where((m - i == t)[None], tap, across)
    down, across = down.astype(jnp.bfloat16), across.astype(jnp.bfloat16)
    tiles = COL_TILE // LANES
    window = COL_TILE + 2 * LANES
    pieces = []
    for tile in range(tiles):
        start = LANES - width + tile * LANES
        pieces.append(jnp.pad(down, ((0, 0), (start, window - start - span), (0, 0))))
    return across, jnp.concatenate(pieces, axis=2)


def smooth_kernel(order_ref, x_ref, before_ref, after_ref, rows_ref, cols_ref, taper_ref, out_ref, y_ref, acc_ref):
    step = pl.program_id(0)
    tiles = pl.num_programs(0) - 1
    corr, scales, rows = x_ref.shape[0], x_ref.shape[1], x_ref.shape[2]
    width = before_ref.shape[2]
    targets = out_ref.shape[0]

    @pl.when(step == 0)
    def _():
        y_ref[:, :, 0:COL_TILE] = jnp.zeros((scales, corr * rows, COL_TILE), y_ref.dtype)
        acc_ref[...] = jnp.zeros_like(acc_ref)

    lane = pl.multiple_of((step + 1) * COL_TILE, COL_TILE)

    @pl.when(step == tiles)
    def _():
        y_ref[:, :, pl.ds(lane, COL_TILE)] = jnp.zeros((scales, corr * rows, COL_TILE), y_ref.dtype)

    @pl.when(step < tiles)
    def _():
        for c in range(corr):
            for s in range(scales):
                full = jnp.concatenate([before_ref[c, s], x_ref[c, s], after_ref[c, s]], axis=0)
                for b in range(rows // LANES):
                    part = full[b * LANES : (b + 1) * LANES + 2 * width]
                    y = jnp.dot(rows_ref[s], part, preferred_element_type=jnp.float32)
                    at = c * rows + b * LANES
                    y_ref[s, at : at + LANES, pl.ds(lane, COL_TILE)] = y.astype(y_ref.dtype)

    @pl.when(step > 0)
    def _():
        first = pl.multiple_of(step * COL_TILE - LANES, LANES)
        smoothed = jnp.zeros((corr * rows, COL_TILE), jnp.float32)
        for s in range(scales):
            smoothed += jnp.dot(
                y_ref[s, :, pl.ds(first, COL_TILE + 2 * LANES)],
                cols_ref[s],
                preferred_element_type=jnp.float32,
            )
        acc_ref[...] += jnp.dot(
            smoothed.astype(jnp.bfloat16), taper_ref[...], preferred_element_type=jnp.float32
        )

    @pl.when(step == tiles)
    def _():
        for d in range(targets):
            at = pl.multiple_of(order_ref[d] * LANES, LANES)
            for c in range(corr):
                out_ref[d, c] = acc_ref[c * rows : (c + 1) * rows, pl.ds(at, LANES)].astype(out_ref.dtype)


def column_products(comp, before, after, kernels, taper, order):
    corr, scales, rows, side = comp.shape
    width = before.shape[2]
    across, down = band_matrices(kernels)
    tiles = side // COL_TILE
    wide = taper.shape[1]
    targets = wide // LANES
    last = tiles - 1

    def ahead(j, order):
        return (0, 0, 0, jnp.minimum(j, last))

    return pl.pallas_call(
        smooth_kernel,
        grid_spec=pltpu.PrefetchScalarGridSpec(
            num_scalar_prefetch=1,
            grid=(tiles + 1,),
            in_specs=[
                pl.BlockSpec((corr, scales, rows, COL_TILE), ahead),
                pl.BlockSpec((corr, scales, width, COL_TILE), ahead),
                pl.BlockSpec((corr, scales, width, COL_TILE), ahead),
                pl.BlockSpec(across.shape, lambda j, order: (0, 0, 0)),
                pl.BlockSpec(down.shape, lambda j, order: (0, 0, 0)),
                pl.BlockSpec((COL_TILE, wide), lambda j, order: (jnp.maximum(j - 1, 0), 0)),
            ],
            out_specs=pl.BlockSpec((targets, corr, rows, LANES), lambda j, order: (0, 0, 0, 0)),
            scratch_shapes=[
                pltpu.VMEM((scales, corr * rows, side + 2 * COL_TILE), jnp.bfloat16),
                pltpu.VMEM((corr * rows, wide), jnp.float32),
            ],
        ),
        out_shape=jax.ShapeDtypeStruct((targets, corr, rows, LANES), jnp.bfloat16),
        compiler_params=pltpu.CompilerParams(
            dimension_semantics=("arbitrary",), vmem_limit_bytes=60 * 1024 * 1024
        ),
        name="column_products",
    )(order, comp, before, after, across, down, taper)


def looked_up(row, index):
    low, high = index % LANES, index // LANES
    out = None
    for chunk in range(row.shape[1] // LANES):
        table = jnp.broadcast_to(row[:, chunk * LANES : (chunk + 1) * LANES], index.shape)
        got = jnp.take_along_axis(table, low, axis=1, mode="promise_in_bounds")
        out = got if out is None else jnp.where(high == chunk, got, out)
    return out


def gain_kernel(gains_ref, index_ref, out_ref):
    p, q = index_ref[:, 0, :], index_ref[:, 1, :]
    for c in range(gains_ref.shape[0]):
        row = gains_ref[c : c + 1, :]
        out_ref[:, c, :] = looked_up(row, p) * looked_up(row, q)


def gain_products(gains, index):
    rows = index.shape[0]
    step = min(rows, 128)
    return pl.pallas_call(
        gain_kernel,
        grid=(rows // step,),
        in_specs=[
            pl.BlockSpec(gains.shape, lambda j: (0, 0)),
            pl.BlockSpec((step,) + index.shape[1:], lambda j: (j, 0, 0)),
        ],
        out_specs=pl.BlockSpec((step, gains.shape[0], index.shape[2]), lambda j: (j, 0, 0)),
        out_shape=jax.ShapeDtypeStruct((rows, gains.shape[0], index.shape[2]), jnp.float32),
        name="gain_products",
    )(gains, index)


def window_weights(corner, offset, grid_side, tile_side):
    places = jnp.arange(grid_side, dtype=jnp.int32)
    relative = places[None, :] - corner[:, None]
    inside = (relative >= 0) & (relative < tile_side)
    delta = (relative.astype(jnp.float32)[:, None, :] - offset[:, :, None]) / KERNEL_WIDTH
    return jnp.where(inside[:, None, :], jnp.exp(-0.5 * delta * delta), 0.0)


def inverse_of(perm):
    count = perm.shape[0]
    places = jnp.arange(count, dtype=jnp.int32)
    return jnp.sum(jnp.where(perm[None, :] == places[:, None], places[None, :], 0), axis=1)


def on_device(
    sky_components,
    scale_kernels,
    row_taper,
    col_taper,
    finish_rows,
    finish_cols,
    subgrid_owner,
    block_cell,
    vis_offset,
    block_owner,
    observed,
    antenna_pair_index,
    gains,
):
    n_facet = lax.axis_size("facet")
    n_strip = lax.axis_size("strip")
    devices = n_facet * n_strip
    comp = sky_components[0]
    corr = comp.shape[0]
    rows = comp.shape[2]
    facet_side = comp.shape[3]
    contrib_side = finish_cols.shape[2]
    grid_side = finish_cols.shape[1]
    sub_rows = row_taper.shape[2] // contrib_side
    sub_cols = col_taper.shape[2] // contrib_side
    width = (scale_kernels.shape[1] - 1) // 2
    tile_side = TILE
    before, after = halo_rows(comp, "strip", 2, width)
    col_perm = subgrid_owner[:sub_cols] % n_strip
    row_perm = subgrid_owner[jnp.arange(sub_rows, dtype=jnp.int32) * sub_cols] // n_strip
    col_inverse = inverse_of(col_perm)
    row_inverse = inverse_of(row_perm)
    by_target = column_products(comp, before, after, scale_kernels, col_taper[0], col_inverse)
    regrouped = lax.all_to_all(by_target, "strip", split_axis=0, concat_axis=0, tiled=True)
    all_rows = row_taper[0].reshape(n_strip, rows, sub_rows, contrib_side)
    finished = jnp.einsum(
        "xrai,xcrj->acij", all_rows, regrouped, preferred_element_type=jnp.float32
    ).astype(jnp.bfloat16)
    outgoing = jnp.take(finished, row_inverse, axis=0)
    mine = lax.all_to_all(outgoing, "facet", split_axis=0, concat_axis=0, tiled=True)
    spread = jnp.einsum(
        "fcij,fsj->fcis", mine, finish_cols, preferred_element_type=jnp.float32
    ).astype(jnp.bfloat16)
    subgrid = jnp.einsum(
        "fri,fcis->crs", finish_rows, spread, preferred_element_type=jnp.float32
    ).astype(jnp.bfloat16)
    blocks = block_owner.shape[0]
    group = min(blocks, 32)
    visibility_block = observed.shape[2]

    def predict_group(pieces):
        cells, offsets = pieces
        row_weights = window_weights(cells[:, 0], offsets[:, 0, :], grid_side, tile_side).astype(
            jnp.bfloat16
        )
        col_weights = window_weights(cells[:, 1], offsets[:, 1, :], grid_side, tile_side)
        along = jnp.einsum(
            "kvx,cxy->kcvy", row_weights, subgrid, preferred_element_type=jnp.float32
        )
        return jnp.sum(along * col_weights[:, None, :, :], axis=3)

    grouped_cells = block_cell.reshape(blocks // group, group, 2)
    grouped_offsets = vis_offset.reshape(blocks // group, group, 2, visibility_block)
    predicted = lax.map(predict_group, (grouped_cells, grouped_offsets)).reshape(
        blocks, corr * visibility_block
    )
    dest = block_owner[:, 0]
    same = dest[:, None] == dest[None, :]
    order = jnp.arange(blocks, dtype=jnp.int32)
    earlier = order[None, :] < order[:, None]
    rank = jnp.sum((same & earlier).astype(jnp.int32), axis=1)
    capacity = observed.shape[0] // devices
    target = dest * capacity + rank
    slots = jnp.arange(devices * capacity, dtype=jnp.int32)
    placing = (slots[:, None] == target[None, :]).astype(jnp.float32)
    outgoing_vis = jnp.dot(
        placing, predicted, precision=lax.Precision.HIGHEST, preferred_element_type=jnp.float32
    )
    outgoing_vis = outgoing_vis.reshape(devices, capacity, corr, visibility_block)
    arrived = lax.all_to_all(
        outgoing_vis.astype(jnp.bfloat16),
        ("facet", "strip"),
        split_axis=0,
        concat_axis=0,
        tiled=True,
    ).astype(outgoing_vis.dtype)
    placed = arrived.reshape(devices * capacity, corr, visibility_block)
    product = gain_products(gains, antenna_pair_index)
    residual = observed - product * placed
    return (subgrid[None], residual)


def solution(mesh):
    placed = (
        P("facet", None, None, "strip", None),
        P(),
        P("facet", None, None),
        P("facet", None, None),
        P(),
        P(),
        P(),
        P(("facet", "strip"), None),
        P(("facet", "strip"), None, None),
        P(("facet", "strip"), None),
        P(("facet", "strip"), None, None),
        P(("facet", "strip"), None, None),
        P(),
    )
    return jax.shard_map(
        on_device,
        mesh=mesh,
        in_specs=placed,
        out_specs=(P(("facet", "strip"), None, None, None), P(("facet", "strip"), None, None)),
        check_vma=False,
    )
```

```python
import jax
import jax.numpy as jnp
from jax import lax
from jax.experimental import pallas as pl
from jax.experimental.pallas import tpu as pltpu
from jax.sharding import PartitionSpec as P

TILE = 32


KERNEL_WIDTH = 1.5


LANES = 128
COL_TILE = 256


def halo_rows(x, axis, dim, width):
    count, length = (lax.axis_size(axis), x.shape[dim])
    up = [(i, (i + 1) % count) for i in range(count - 1)]
    down = [(j, i) for i, j in up]
    last = lax.slice_in_dim(x, length - width, length, axis=dim)
    initial = lax.slice_in_dim(x, 0, width, axis=dim)
    return lax.ppermute(last, axis, up), lax.ppermute(initial, axis, down)


def band_matrices(kernels):
    taps = kernels.shape[1]
    width = (taps - 1) // 2
    span = LANES + taps - 1
    k = lax.broadcasted_iota(jnp.int32, (span, LANES), 0)
    n = lax.broadcasted_iota(jnp.int32, (span, LANES), 1)
    i = lax.broadcasted_iota(jnp.int32, (LANES, span), 0)
    m = lax.broadcasted_iota(jnp.int32, (LANES, span), 1)
    down = jnp.zeros((kernels.shape[0], span, LANES), jnp.float32)
    across = jnp.zeros((kernels.shape[0], LANES, span), jnp.float32)
    for t in range(taps):
        tap = kernels[:, t][:, None, None]
        down = jnp.where((k - n == t)[None], tap, down)
        across = jnp.where((m - i == t)[None], tap, across)
    down, across = down.astype(jnp.bfloat16), across.astype(jnp.bfloat16)
    tiles = COL_TILE // LANES
    window = COL_TILE + 2 * LANES
    pieces = []
    for tile in range(tiles):
        start = LANES - width + tile * LANES
        pieces.append(jnp.pad(down, ((0, 0), (start, window - start - span), (0, 0))))
    return across, jnp.concatenate(pieces, axis=2)


def smooth_kernel(order_ref, x_ref, before_ref, after_ref, rows_ref, cols_ref, taper_ref, out_ref, y_ref, acc_ref):
    step = pl.program_id(0)
    tiles = pl.num_programs(0) - 1
    corr, scales, rows = x_ref.shape[0], x_ref.shape[1], x_ref.shape[2]
    width = before_ref.shape[2]
    targets = out_ref.shape[0]

    @pl.when(step == 0)
    def _():
        y_ref[:, :, 0:COL_TILE] = jnp.zeros((scales, corr * rows, COL_TILE), y_ref.dtype)
        acc_ref[...] = jnp.zeros_like(acc_ref)

    lane = pl.multiple_of((step + 1) * COL_TILE, COL_TILE)

    @pl.when(step == tiles)
    def _():
        y_ref[:, :, pl.ds(lane, COL_TILE)] = jnp.zeros((scales, corr * rows, COL_TILE), y_ref.dtype)

    @pl.when(step < tiles)
    def _():
        for c in range(corr):
            for s in range(scales):
                full = jnp.concatenate([before_ref[c, s], x_ref[c, s], after_ref[c, s]], axis=0)
                for b in range(rows // LANES):
                    part = full[b * LANES : (b + 1) * LANES + 2 * width]
                    y = jnp.dot(rows_ref[s], part, preferred_element_type=jnp.float32)
                    at = c * rows + b * LANES
                    y_ref[s, at : at + LANES, pl.ds(lane, COL_TILE)] = y.astype(y_ref.dtype)

    @pl.when(step > 0)
    def _():
        first = pl.multiple_of(step * COL_TILE - LANES, LANES)
        smoothed = jnp.zeros((corr * rows, COL_TILE), jnp.float32)
        for s in range(scales):
            smoothed += jnp.dot(
                y_ref[s, :, pl.ds(first, COL_TILE + 2 * LANES)],
                cols_ref[s],
                preferred_element_type=jnp.float32,
            )
        acc_ref[...] += jnp.dot(
            smoothed.astype(jnp.bfloat16), taper_ref[...], preferred_element_type=jnp.float32
        )

    @pl.when(step == tiles)
    def _():
        for d in range(targets):
            at = pl.multiple_of(order_ref[d] * LANES, LANES)
            for c in range(corr):
                out_ref[d, c] = acc_ref[c * rows : (c + 1) * rows, pl.ds(at, LANES)].astype(out_ref.dtype)


def column_products(comp, before, after, kernels, taper, order):
    corr, scales, rows, side = comp.shape
    width = before.shape[2]
    across, down = band_matrices(kernels)
    tiles = side // COL_TILE
    wide = taper.shape[1]
    targets = wide // LANES
    last = tiles - 1

    def ahead(j, order):
        return (0, 0, 0, jnp.minimum(j, last))

    return pl.pallas_call(
        smooth_kernel,
        grid_spec=pltpu.PrefetchScalarGridSpec(
            num_scalar_prefetch=1,
            grid=(tiles + 1,),
            in_specs=[
                pl.BlockSpec((corr, scales, rows, COL_TILE), ahead),
                pl.BlockSpec((corr, scales, width, COL_TILE), ahead),
                pl.BlockSpec((corr, scales, width, COL_TILE), ahead),
                pl.BlockSpec(across.shape, lambda j, order: (0, 0, 0)),
                pl.BlockSpec(down.shape, lambda j, order: (0, 0, 0)),
                pl.BlockSpec((COL_TILE, wide), lambda j, order: (jnp.maximum(j - 1, 0), 0)),
            ],
            out_specs=pl.BlockSpec((targets, corr, rows, LANES), lambda j, order: (0, 0, 0, 0)),
            scratch_shapes=[
                pltpu.VMEM((scales, corr * rows, side + 2 * COL_TILE), jnp.bfloat16),
                pltpu.VMEM((corr * rows, wide), jnp.float32),
            ],
        ),
        out_shape=jax.ShapeDtypeStruct((targets, corr, rows, LANES), jnp.bfloat16),
        compiler_params=pltpu.CompilerParams(
            dimension_semantics=("arbitrary",), vmem_limit_bytes=60 * 1024 * 1024
        ),
        name="column_products",
    )(order, comp, before, after, across, down, taper)


def looked_up(row, index):
    low, high = index % LANES, index // LANES
    out = None
    for chunk in range(row.shape[1] // LANES):
        table = jnp.broadcast_to(row[:, chunk * LANES : (chunk + 1) * LANES], index.shape)
        got = jnp.take_along_axis(table, low, axis=1, mode="promise_in_bounds")
        out = got if out is None else jnp.where(high == chunk, got, out)
    return out


def gain_kernel(gains_ref, index_ref, out_ref):
    p, q = index_ref[:, 0, :], index_ref[:, 1, :]
    for c in range(gains_ref.shape[0]):
        row = gains_ref[c : c + 1, :]
        out_ref[:, c, :] = looked_up(row, p) * looked_up(row, q)


def gain_products(gains, index):
    rows = index.shape[0]
    step = min(rows, 128)
    return pl.pallas_call(
        gain_kernel,
        grid=(rows // step,),
        in_specs=[
            pl.BlockSpec(gains.shape, lambda j: (0, 0)),
            pl.BlockSpec((step,) + index.shape[1:], lambda j: (j, 0, 0)),
        ],
        out_specs=pl.BlockSpec((step, gains.shape[0], index.shape[2]), lambda j: (j, 0, 0)),
        out_shape=jax.ShapeDtypeStruct((rows, gains.shape[0], index.shape[2]), jnp.float32),
        name="gain_products",
    )(gains, index)


ALIGN = 16


def degrid_kernel(corner_ref, target_ref, mine_ref, cols_ref, rows_ref, offset_ref, subgrid_ref, out_ref, turned_ref):
    facets, corr = mine_ref.shape[0], mine_ref.shape[1]
    side = cols_ref.shape[1]
    blocks, vis = offset_ref.shape[0], offset_ref.shape[2]
    tall, wide = TILE + ALIGN, 2 * LANES
    row_mats = jnp.concatenate([rows_ref[f] for f in range(facets)], axis=1)
    across = (((1,), (1,)), ((), ()))
    for c in range(corr):
        spread = jnp.concatenate(
            [
                lax.dot_general(
                    cols_ref[f], mine_ref[f, c], across, preferred_element_type=jnp.float32
                ).astype(jnp.bfloat16)
                for f in range(facets)
            ],
            axis=1,
        )
        subgrid_ref[c] = lax.dot_general(
            row_mats, spread, across, preferred_element_type=jnp.float32
        ).astype(jnp.bfloat16)
        turned_ref[c] = lax.dot_general(
            spread, row_mats, across, preferred_element_type=jnp.float32
        ).astype(jnp.bfloat16)
    out_ref[...] = jnp.zeros_like(out_ref)
    row_places = lax.broadcasted_iota(jnp.int32, (wide, vis), 0)
    col_places = lax.broadcasted_iota(jnp.int32, (tall, vis), 0)
    factor = -0.5 / (KERNEL_WIDTH * KERNEL_WIDTH)

    def weights(places, offset):
        delta = places.astype(jnp.float32) - offset
        inside = (places >= 0) & (places < TILE)
        return jnp.where(inside, jnp.exp(factor * (delta * delta)), 0.0)

    def one_block(k, carry):
        r, q = corner_ref[k, 0], corner_ref[k, 1]
        r0 = pl.multiple_of(jnp.minimum(r // LANES * LANES, side - wide), LANES)
        q0 = pl.multiple_of(jnp.minimum(q // ALIGN * ALIGN, side - tall), ALIGN)
        offsets = offset_ref[k]
        row_weights = weights(row_places - (r - r0), offsets[0:1]).astype(jnp.bfloat16)
        col_weights = weights(col_places - (q - q0), offsets[1:2])
        tile = jnp.concatenate(
            [turned_ref[c, pl.ds(q0, tall), pl.ds(r0, wide)] for c in range(corr)], axis=0
        )
        along = jnp.dot(tile, row_weights, preferred_element_type=jnp.float32)
        values = [
            jnp.sum(along[c * tall : (c + 1) * tall] * col_weights, axis=0, keepdims=True)
            for c in range(corr)
        ]
        out_ref[target_ref[k]] = jnp.concatenate(values, axis=0).astype(out_ref.dtype)
        return carry

    lax.fori_loop(0, blocks, one_block, 0, unroll=4)


def formed_and_predicted(mine, finish_cols, finish_rows, corners, offsets, target, slots):
    corr = mine.shape[1]
    side = finish_cols.shape[1]
    vis = offsets.shape[2]
    whole = pl.BlockSpec(memory_space=pltpu.VMEM)
    scalars = pl.BlockSpec(memory_space=pltpu.SMEM)
    return pl.pallas_call(
        degrid_kernel,
        in_specs=[scalars, scalars, whole, whole, whole, whole],
        out_specs=[whole, whole],
        out_shape=[
            jax.ShapeDtypeStruct((corr, side, side), jnp.bfloat16),
            jax.ShapeDtypeStruct((slots, corr, vis), jnp.bfloat16),
        ],
        scratch_shapes=[pltpu.VMEM((corr, side, side), jnp.bfloat16)],
        compiler_params=pltpu.CompilerParams(vmem_limit_bytes=32 * 1024 * 1024),
        name="formed_and_predicted",
    )(corners, target, mine, finish_cols, finish_rows, offsets)


def inverse_of(perm):
    count = perm.shape[0]
    places = jnp.arange(count, dtype=jnp.int32)
    return jnp.sum(jnp.where(perm[None, :] == places[:, None], places[None, :], 0), axis=1)


def on_device(
    sky_components,
    scale_kernels,
    row_taper,
    col_taper,
    finish_rows,
    finish_cols,
    subgrid_owner,
    block_cell,
    vis_offset,
    block_owner,
    observed,
    antenna_pair_index,
    gains,
):
    n_facet = lax.axis_size("facet")
    n_strip = lax.axis_size("strip")
    devices = n_facet * n_strip
    comp = sky_components[0]
    corr = comp.shape[0]
    rows = comp.shape[2]
    facet_side = comp.shape[3]
    contrib_side = finish_cols.shape[2]
    sub_rows = row_taper.shape[2] // contrib_side
    sub_cols = col_taper.shape[2] // contrib_side
    width = (scale_kernels.shape[1] - 1) // 2
    before, after = halo_rows(comp, "strip", 2, width)
    col_perm = subgrid_owner[:sub_cols] % n_strip
    row_perm = subgrid_owner[jnp.arange(sub_rows, dtype=jnp.int32) * sub_cols] // n_strip
    col_inverse = inverse_of(col_perm)
    row_inverse = inverse_of(row_perm)
    by_target = column_products(comp, before, after, scale_kernels, col_taper[0], col_inverse)
    regrouped = lax.all_to_all(by_target, "strip", split_axis=0, concat_axis=0, tiled=True)
    all_rows = row_taper[0].reshape(n_strip, rows, sub_rows, contrib_side)
    finished = jnp.einsum(
        "xrai,xcrj->acij", all_rows, regrouped, preferred_element_type=jnp.float32
    ).astype(jnp.bfloat16)
    outgoing = jnp.take(finished, row_inverse, axis=0)
    mine = lax.all_to_all(outgoing, "facet", split_axis=0, concat_axis=0, tiled=True)
    blocks = block_owner.shape[0]
    visibility_block = observed.shape[2]
    dest = block_owner[:, 0]
    same = dest[:, None] == dest[None, :]
    order = jnp.arange(blocks, dtype=jnp.int32)
    earlier = order[None, :] < order[:, None]
    rank = jnp.sum((same & earlier).astype(jnp.int32), axis=1)
    capacity = observed.shape[0] // devices
    target = dest * capacity + rank
    subgrid, outgoing_vis = formed_and_predicted(
        mine, finish_cols, finish_rows, block_cell, vis_offset, target, devices * capacity
    )
    outgoing_vis = outgoing_vis.reshape(devices, capacity, corr, visibility_block)
    arrived = lax.all_to_all(
        outgoing_vis, ("facet", "strip"), split_axis=0, concat_axis=0, tiled=True
    ).astype(jnp.float32)
    placed = arrived.reshape(devices * capacity, corr, visibility_block)
    product = gain_products(gains, antenna_pair_index)
    residual = observed - product * placed
    return (subgrid[None], residual)


def solution(mesh):
    placed = (
        P("facet", None, None, "strip", None),
        P(),
        P("facet", None, None),
        P("facet", None, None),
        P(),
        P(),
        P(),
        P(("facet", "strip"), None),
        P(("facet", "strip"), None, None),
        P(("facet", "strip"), None),
        P(("facet", "strip"), None, None),
        P(("facet", "strip"), None, None),
        P(),
    )
    return jax.shard_map(
        on_device,
        mesh=mesh,
        in_specs=placed,
        out_specs=(P(("facet", "strip"), None, None, None), P(("facet", "strip"), None, None)),
        check_vma=False,
    )
```

```python
import functools

import jax
import jax.numpy as jnp
from jax import lax
from jax.experimental import pallas as pl
from jax.experimental.pallas import tpu as pltpu
from jax.sharding import PartitionSpec as P

TILE = 32


KERNEL_WIDTH = 1.5


LANES = 128
COL_TILE = 256
MESH = pl.DeviceIdType.MESH


def fill_bands(taps_ref, across_ref, down_ref, width):
    scales, taps = taps_ref.shape
    span = LANES + taps - 1
    k = lax.broadcasted_iota(jnp.int32, (span, LANES), 0)
    n = lax.broadcasted_iota(jnp.int32, (span, LANES), 1)
    i = lax.broadcasted_iota(jnp.int32, (LANES, span), 0)
    m = lax.broadcasted_iota(jnp.int32, (LANES, span), 1)
    down_ref[...] = jnp.zeros_like(down_ref)
    for s in range(scales):

        def one_tap(t, carry, s=s):
            down, across = carry
            tap = taps_ref[s, t]
            return jnp.where(k - n == t, tap, down), jnp.where(m - i == t, tap, across)

        down, across = lax.fori_loop(
            0,
            taps,
            one_tap,
            (jnp.zeros((span, LANES), jnp.float32), jnp.zeros((LANES, span), jnp.float32)),
            unroll=3,
        )
        across_ref[s] = across.astype(across_ref.dtype)
        down = down.astype(down_ref.dtype)
        for tile in range(COL_TILE // LANES):
            start = LANES - width + tile * LANES
            down_ref[s, start : start + span, tile * LANES : (tile + 1) * LANES] = down


def smooth_kernel(count, order_ref, taps_ref, x_ref, taper_in, out_ref, x_buf, taper_ref, across_ref, down_ref, y_ref, smooth_ref, acc_ref, stage_ref, local_sem, taper_sem, halo_send, halo_recv, send_sem, recv_sem):
    corr, scales, rows, side = x_ref.shape
    width = (taps_ref.shape[1] - 1) // 2
    tiles = side // COL_TILE
    me = lax.axis_index("strip")
    right, left = lax.rem(me + 1, count), lax.rem(me + count - 1, count)
    loads = [
        pltpu.make_async_copy(x_ref.at[c], x_buf.at[c, :, pl.ds(width, rows)], local_sem.at[c])
        for c in range(corr)
    ]
    taper_load = pltpu.make_async_copy(taper_in, taper_ref, taper_sem)
    for load in loads:
        load.start()
    taper_load.start()
    barrier = pltpu.get_barrier_semaphore()
    for off in range(1, count):
        pl.semaphore_signal(
            barrier, inc=1, device_id={"strip": lax.rem(me + off, count)}, device_id_type=MESH
        )
    pl.semaphore_wait(barrier, count - 1)
    halos = []
    for c in range(corr):
        pair = []
        for way, (start, landing, peer) in enumerate(
            ((rows - width, 0, right), (0, rows + width, left))
        ):
            pair.append(
                pltpu.make_async_remote_copy(
                    src_ref=x_ref.at[c, :, pl.ds(start, width)],
                    dst_ref=x_buf.at[c, :, pl.ds(landing, width)],
                    send_sem=halo_send.at[c, way],
                    recv_sem=halo_recv.at[c, way],
                    device_id={"strip": peer},
                    device_id_type=MESH,
                )
            )
        for copy in pair:
            copy.start()
        halos.append(pair)
    fill_bands(taps_ref, across_ref, down_ref, width)
    y_ref[:, :, 0:LANES] = jnp.zeros((scales, rows, LANES), y_ref.dtype)
    y_ref[:, :, LANES + side : 2 * LANES + side] = jnp.zeros((scales, rows, LANES), y_ref.dtype)
    sends = []
    for c in range(corr):
        loads[c].wait()
        for copy in halos[c]:
            copy.wait()

        @pl.when(me == 0)
        def _():
            x_buf[c, :, 0:width] = jnp.zeros((scales, width, side), x_buf.dtype)

        @pl.when(me == count - 1)
        def _():
            x_buf[c, :, rows + width : rows + 2 * width] = jnp.zeros((scales, width, side), x_buf.dtype)

        for s in range(scales):
            for b in range(rows // LANES):
                part = x_buf[c, s, b * LANES : (b + 1) * LANES + 2 * width]
                y = jnp.dot(across_ref[s], part, preferred_element_type=jnp.float32)
                y_ref[s, b * LANES : (b + 1) * LANES, LANES : LANES + side] = y.astype(y_ref.dtype)

        def one_tile(tile, carry):
            first = pl.multiple_of(tile * COL_TILE, COL_TILE)
            smoothed = jnp.zeros((rows, COL_TILE), jnp.float32)
            for s in range(scales):
                smoothed += jnp.dot(
                    y_ref[s, :, pl.ds(first, COL_TILE + 2 * LANES)],
                    down_ref[s],
                    preferred_element_type=jnp.float32,
                )
            smooth_ref[:, pl.ds(first, COL_TILE)] = smoothed.astype(smooth_ref.dtype)
            return carry

        lax.fori_loop(0, tiles, one_tile, 0, unroll=2)
        if c == 0:
            taper_load.wait()
        acc = jnp.dot(smooth_ref[...], taper_ref[...], preferred_element_type=jnp.float32)
        for d in range(count):
            acc_ref[d] = acc[:, d * LANES : (d + 1) * LANES]
        for d in range(count):
            stage_ref[c, d] = acc_ref[order_ref[d]].astype(stage_ref.dtype)
        for off in range(1, count):
            peer = lax.rem(me + off, count)
            copy = pltpu.make_async_remote_copy(
                src_ref=stage_ref.at[c, peer],
                dst_ref=out_ref.at[me, c],
                send_sem=send_sem.at[c, off],
                recv_sem=recv_sem.at[c, off],
                device_id={"strip": peer},
                device_id_type=MESH,
            )
            copy.start()
            sends.append(copy)
        out_ref[me, c] = stage_ref[c, me]
    for copy in sends:
        copy.wait()


def regrouped_products(comp, kernels, taper, order):
    corr, scales, rows, side = comp.shape
    taps = kernels.shape[1]
    count = lax.axis_size("strip")
    whole = pl.BlockSpec(memory_space=pltpu.VMEM)
    scalars = pl.BlockSpec(memory_space=pltpu.SMEM)
    remote = pl.BlockSpec(memory_space=pl.ANY)
    return pl.pallas_call(
        functools.partial(smooth_kernel, count),
        in_specs=[scalars, scalars, remote, remote],
        out_specs=whole,
        scratch_shapes=[
            pltpu.VMEM((corr, scales, rows + taps - 1, side), jnp.bfloat16),
            pltpu.VMEM(taper.shape, jnp.bfloat16),
            pltpu.VMEM((scales, LANES, LANES + taps - 1), jnp.bfloat16),
            pltpu.VMEM((scales, COL_TILE + 2 * LANES, COL_TILE), jnp.bfloat16),
            pltpu.VMEM((scales, rows, side + 2 * LANES), jnp.bfloat16),
            pltpu.VMEM((rows, side), jnp.bfloat16),
            pltpu.VMEM((count, rows, LANES), jnp.float32),
            pltpu.VMEM((corr, count, rows, LANES), jnp.bfloat16),
            pltpu.SemaphoreType.DMA((corr,)),
            pltpu.SemaphoreType.DMA,
            pltpu.SemaphoreType.DMA((corr, 2)),
            pltpu.SemaphoreType.DMA((corr, 2)),
            pltpu.SemaphoreType.DMA((corr, count)),
            pltpu.SemaphoreType.DMA((corr, count)),
        ],
        out_shape=jax.ShapeDtypeStruct((count, corr, rows, LANES), jnp.bfloat16),
        compiler_params=pltpu.CompilerParams(
            collective_id=0, has_side_effects=True, vmem_limit_bytes=60 * 1024 * 1024
        ),
        name="regrouped_products",
    )(order, kernels, comp, taper)


def looked_up(row, index):
    low, high = index % LANES, index // LANES
    out = None
    for chunk in range(row.shape[1] // LANES):
        table = jnp.broadcast_to(row[:, chunk * LANES : (chunk + 1) * LANES], index.shape)
        got = jnp.take_along_axis(table, low, axis=1, mode="promise_in_bounds")
        out = got if out is None else jnp.where(high == chunk, got, out)
    return out


def gain_kernel(gains_ref, index_ref, out_ref):
    p, q = index_ref[:, 0, :], index_ref[:, 1, :]
    for c in range(gains_ref.shape[0]):
        row = gains_ref[c : c + 1, :]
        out_ref[:, c, :] = looked_up(row, p) * looked_up(row, q)


def gain_products(gains, index):
    rows = index.shape[0]
    step = min(rows, 128)
    return pl.pallas_call(
        gain_kernel,
        grid=(rows // step,),
        in_specs=[
            pl.BlockSpec(gains.shape, lambda j: (0, 0)),
            pl.BlockSpec((step,) + index.shape[1:], lambda j: (j, 0, 0)),
        ],
        out_specs=pl.BlockSpec((step, gains.shape[0], index.shape[2]), lambda j: (j, 0, 0)),
        out_shape=jax.ShapeDtypeStruct((rows, gains.shape[0], index.shape[2]), jnp.float32),
        name="gain_products",
    )(gains, index)


ALIGN = 16


def degrid_kernel(corner_ref, target_ref, mine_ref, cols_ref, rows_ref, offset_ref, subgrid_ref, out_ref, turned_ref):
    facets, corr = mine_ref.shape[0], mine_ref.shape[1]
    side = cols_ref.shape[1]
    blocks, vis = offset_ref.shape[0], offset_ref.shape[2]
    tall, wide = TILE + ALIGN, 2 * LANES
    row_mats = jnp.concatenate([rows_ref[f] for f in range(facets)], axis=1)
    across = (((1,), (1,)), ((), ()))
    for c in range(corr):
        spread = jnp.concatenate(
            [
                lax.dot_general(
                    cols_ref[f], mine_ref[f, c], across, preferred_element_type=jnp.float32
                ).astype(jnp.bfloat16)
                for f in range(facets)
            ],
            axis=1,
        )
        subgrid_ref[c] = lax.dot_general(
            row_mats, spread, across, preferred_element_type=jnp.float32
        ).astype(jnp.bfloat16)
        turned_ref[c] = lax.dot_general(
            spread, row_mats, across, preferred_element_type=jnp.float32
        ).astype(jnp.bfloat16)
    out_ref[...] = jnp.zeros_like(out_ref)
    row_places = lax.broadcasted_iota(jnp.int32, (wide, vis), 0)
    col_places = lax.broadcasted_iota(jnp.int32, (tall, vis), 0)
    factor = -0.5 / (KERNEL_WIDTH * KERNEL_WIDTH)

    def weights(places, offset):
        delta = places.astype(jnp.float32) - offset
        inside = (places >= 0) & (places < TILE)
        return jnp.where(inside, jnp.exp(factor * (delta * delta)), 0.0)

    def one_block(k, carry):
        r, q = corner_ref[k, 0], corner_ref[k, 1]
        r0 = pl.multiple_of(jnp.minimum(r // LANES * LANES, side - wide), LANES)
        q0 = pl.multiple_of(jnp.minimum(q // ALIGN * ALIGN, side - tall), ALIGN)
        offsets = offset_ref[k]
        row_weights = weights(row_places - (r - r0), offsets[0:1]).astype(jnp.bfloat16)
        col_weights = weights(col_places - (q - q0), offsets[1:2])
        tile = jnp.concatenate(
            [turned_ref[c, pl.ds(q0, tall), pl.ds(r0, wide)] for c in range(corr)], axis=0
        )
        along = jnp.dot(tile, row_weights, preferred_element_type=jnp.float32)
        values = [
            jnp.sum(along[c * tall : (c + 1) * tall] * col_weights, axis=0, keepdims=True)
            for c in range(corr)
        ]
        out_ref[target_ref[k]] = jnp.concatenate(values, axis=0).astype(out_ref.dtype)
        return carry

    lax.fori_loop(0, blocks, one_block, 0, unroll=4)


def formed_and_predicted(mine, finish_cols, finish_rows, corners, offsets, target, slots):
    corr = mine.shape[1]
    side = finish_cols.shape[1]
    vis = offsets.shape[2]
    whole = pl.BlockSpec(memory_space=pltpu.VMEM)
    scalars = pl.BlockSpec(memory_space=pltpu.SMEM)
    return pl.pallas_call(
        degrid_kernel,
        in_specs=[scalars, scalars, whole, whole, whole, whole],
        out_specs=[whole, whole],
        out_shape=[
            jax.ShapeDtypeStruct((corr, side, side), jnp.bfloat16),
            jax.ShapeDtypeStruct((slots, corr, vis), jnp.bfloat16),
        ],
        scratch_shapes=[pltpu.VMEM((corr, side, side), jnp.bfloat16)],
        compiler_params=pltpu.CompilerParams(vmem_limit_bytes=32 * 1024 * 1024),
        name="formed_and_predicted",
    )(corners, target, mine, finish_cols, finish_rows, offsets)


def inverse_of(perm):
    count = perm.shape[0]
    places = jnp.arange(count, dtype=jnp.int32)
    return jnp.sum(jnp.where(perm[None, :] == places[:, None], places[None, :], 0), axis=1)


def on_device(
    sky_components,
    scale_kernels,
    row_taper,
    col_taper,
    finish_rows,
    finish_cols,
    subgrid_owner,
    block_cell,
    vis_offset,
    block_owner,
    observed,
    antenna_pair_index,
    gains,
):
    n_facet = lax.axis_size("facet")
    n_strip = lax.axis_size("strip")
    devices = n_facet * n_strip
    comp = sky_components[0]
    corr = comp.shape[0]
    rows = comp.shape[2]
    facet_side = comp.shape[3]
    contrib_side = finish_cols.shape[2]
    sub_rows = row_taper.shape[2] // contrib_side
    sub_cols = col_taper.shape[2] // contrib_side
    col_perm = subgrid_owner[:sub_cols] % n_strip
    row_perm = subgrid_owner[jnp.arange(sub_rows, dtype=jnp.int32) * sub_cols] // n_strip
    col_inverse = inverse_of(col_perm)
    row_inverse = inverse_of(row_perm)
    regrouped = regrouped_products(comp, scale_kernels, col_taper[0], col_inverse)
    all_rows = row_taper[0].reshape(n_strip, rows, sub_rows, contrib_side)
    finished = jnp.einsum(
        "xrai,xcrj->acij", all_rows, regrouped, preferred_element_type=jnp.float32
    ).astype(jnp.bfloat16)
    outgoing = jnp.take(finished, row_inverse, axis=0)
    mine = lax.all_to_all(outgoing, "facet", split_axis=0, concat_axis=0, tiled=True)
    blocks = block_owner.shape[0]
    visibility_block = observed.shape[2]
    dest = block_owner[:, 0]
    same = dest[:, None] == dest[None, :]
    order = jnp.arange(blocks, dtype=jnp.int32)
    earlier = order[None, :] < order[:, None]
    rank = jnp.sum((same & earlier).astype(jnp.int32), axis=1)
    capacity = observed.shape[0] // devices
    target = dest * capacity + rank
    subgrid, outgoing_vis = formed_and_predicted(
        mine, finish_cols, finish_rows, block_cell, vis_offset, target, devices * capacity
    )
    outgoing_vis = outgoing_vis.reshape(devices, capacity, corr, visibility_block)
    arrived = lax.all_to_all(
        outgoing_vis, ("facet", "strip"), split_axis=0, concat_axis=0, tiled=True
    ).astype(jnp.float32)
    placed = arrived.reshape(devices * capacity, corr, visibility_block)
    product = gain_products(gains, antenna_pair_index)
    residual = observed - product * placed
    return (subgrid[None], residual)


def solution(mesh):
    placed = (
        P("facet", None, None, "strip", None),
        P(),
        P("facet", None, None),
        P("facet", None, None),
        P(),
        P(),
        P(),
        P(("facet", "strip"), None),
        P(("facet", "strip"), None, None),
        P(("facet", "strip"), None),
        P(("facet", "strip"), None, None),
        P(("facet", "strip"), None, None),
        P(),
    )
    return jax.shard_map(
        on_device,
        mesh=mesh,
        in_specs=placed,
        out_specs=(P(("facet", "strip"), None, None, None), P(("facet", "strip"), None, None)),
        check_vma=False,
    )
```

```python
import functools

import jax
import jax.numpy as jnp
from jax import lax
from jax.experimental import pallas as pl
from jax.experimental.pallas import tpu as pltpu
from jax.sharding import PartitionSpec as P

TILE = 32


KERNEL_WIDTH = 1.5


LANES = 128
COL_TILE = 256
MESH = pl.DeviceIdType.MESH


def fill_bands(taps_ref, across_ref, down_ref, width):
    scales, taps = taps_ref.shape
    span = LANES + taps - 1
    k = lax.broadcasted_iota(jnp.int32, (span, LANES), 0)
    n = lax.broadcasted_iota(jnp.int32, (span, LANES), 1)
    i = lax.broadcasted_iota(jnp.int32, (LANES, span), 0)
    m = lax.broadcasted_iota(jnp.int32, (LANES, span), 1)
    down_ref[...] = jnp.zeros_like(down_ref)
    for s in range(scales):

        def one_tap(t, carry, s=s):
            down, across = carry
            tap = taps_ref[s, t]
            return jnp.where(k - n == t, tap, down), jnp.where(m - i == t, tap, across)

        down, across = lax.fori_loop(
            0,
            taps,
            one_tap,
            (jnp.zeros((span, LANES), jnp.float32), jnp.zeros((LANES, span), jnp.float32)),
            unroll=3,
        )
        across_ref[s] = across.astype(across_ref.dtype)
        down = down.astype(down_ref.dtype)
        for tile in range(COL_TILE // LANES):
            start = LANES - width + tile * LANES
            down_ref[s, start : start + span, tile * LANES : (tile + 1) * LANES] = down


def smooth_kernel(count, order_ref, taps_ref, x_ref, taper_in, out_ref, x_buf, taper_ref, across_ref, down_ref, y_ref, smooth_ref, acc_ref, stage_ref, local_sem, taper_sem, halo_send, halo_recv, send_sem, recv_sem):
    corr, scales, rows, side = x_ref.shape
    width = (taps_ref.shape[1] - 1) // 2
    tiles = side // COL_TILE
    me = lax.axis_index("strip")
    right, left = lax.rem(me + 1, count), lax.rem(me + count - 1, count)
    loads = [
        pltpu.make_async_copy(x_ref.at[c], x_buf.at[c, :, pl.ds(width, rows)], local_sem.at[c])
        for c in range(corr)
    ]
    taper_load = pltpu.make_async_copy(taper_in, taper_ref, taper_sem)
    for load in loads:
        load.start()
    taper_load.start()
    barrier = pltpu.get_barrier_semaphore()
    for off in range(1, count):
        pl.semaphore_signal(
            barrier, inc=1, device_id={"strip": lax.rem(me + off, count)}, device_id_type=MESH
        )
    pl.semaphore_wait(barrier, count - 1)
    halos = []
    for c in range(corr):
        pair = []
        for way, (start, landing, peer) in enumerate(
            ((rows - width, 0, right), (0, rows + width, left))
        ):
            pair.append(
                pltpu.make_async_remote_copy(
                    src_ref=x_ref.at[c, :, pl.ds(start, width)],
                    dst_ref=x_buf.at[c, :, pl.ds(landing, width)],
                    send_sem=halo_send.at[c, way],
                    recv_sem=halo_recv.at[c, way],
                    device_id={"strip": peer},
                    device_id_type=MESH,
                )
            )
        for copy in pair:
            copy.start()
        halos.append(pair)
    fill_bands(taps_ref, across_ref, down_ref, width)
    y_ref[:, :, 0:LANES] = jnp.zeros((scales, rows, LANES), y_ref.dtype)
    y_ref[:, :, LANES + side : 2 * LANES + side] = jnp.zeros((scales, rows, LANES), y_ref.dtype)
    sends = []
    for c in range(corr):
        loads[c].wait()
        for copy in halos[c]:
            copy.wait()

        @pl.when(me == 0)
        def _():
            x_buf[c, :, 0:width] = jnp.zeros((scales, width, side), x_buf.dtype)

        @pl.when(me == count - 1)
        def _():
            x_buf[c, :, rows + width : rows + 2 * width] = jnp.zeros((scales, width, side), x_buf.dtype)

        for s in range(scales):
            for b in range(rows // LANES):
                part = x_buf[c, s, b * LANES : (b + 1) * LANES + 2 * width]
                y = jnp.dot(across_ref[s], part, preferred_element_type=jnp.float32)
                y_ref[s, b * LANES : (b + 1) * LANES, LANES : LANES + side] = y.astype(y_ref.dtype)

        def one_tile(tile, carry):
            first = pl.multiple_of(tile * COL_TILE, COL_TILE)
            smoothed = jnp.zeros((rows, COL_TILE), jnp.float32)
            for s in range(scales):
                smoothed += jnp.dot(
                    y_ref[s, :, pl.ds(first, COL_TILE + 2 * LANES)],
                    down_ref[s],
                    preferred_element_type=jnp.float32,
                )
            smooth_ref[:, pl.ds(first, COL_TILE)] = smoothed.astype(smooth_ref.dtype)
            return carry

        lax.fori_loop(0, tiles, one_tile, 0, unroll=2)
        if c == 0:
            taper_load.wait()
        acc = jnp.dot(smooth_ref[...], taper_ref[...], preferred_element_type=jnp.float32)
        for d in range(count):
            acc_ref[d] = acc[:, d * LANES : (d + 1) * LANES]
        for d in range(count):
            stage_ref[c, d] = acc_ref[order_ref[d]].astype(stage_ref.dtype)
        for off in range(1, count):
            peer = lax.rem(me + off, count)
            copy = pltpu.make_async_remote_copy(
                src_ref=stage_ref.at[c, peer],
                dst_ref=out_ref.at[me, c],
                send_sem=send_sem.at[c, off],
                recv_sem=recv_sem.at[c, off],
                device_id={"strip": peer},
                device_id_type=MESH,
            )
            copy.start()
            sends.append(copy)
        out_ref[me, c] = stage_ref[c, me]
    for copy in sends:
        copy.wait()


def regrouped_products(comp, kernels, taper, order):
    corr, scales, rows, side = comp.shape
    taps = kernels.shape[1]
    count = lax.axis_size("strip")
    whole = pl.BlockSpec(memory_space=pltpu.VMEM)
    scalars = pl.BlockSpec(memory_space=pltpu.SMEM)
    remote = pl.BlockSpec(memory_space=pl.ANY)
    return pl.pallas_call(
        functools.partial(smooth_kernel, count),
        in_specs=[scalars, scalars, remote, remote],
        out_specs=whole,
        scratch_shapes=[
            pltpu.VMEM((corr, scales, rows + taps - 1, side), jnp.bfloat16),
            pltpu.VMEM(taper.shape, jnp.bfloat16),
            pltpu.VMEM((scales, LANES, LANES + taps - 1), jnp.bfloat16),
            pltpu.VMEM((scales, COL_TILE + 2 * LANES, COL_TILE), jnp.bfloat16),
            pltpu.VMEM((scales, rows, side + 2 * LANES), jnp.bfloat16),
            pltpu.VMEM((rows, side), jnp.bfloat16),
            pltpu.VMEM((count, rows, LANES), jnp.float32),
            pltpu.VMEM((corr, count, rows, LANES), jnp.bfloat16),
            pltpu.SemaphoreType.DMA((corr,)),
            pltpu.SemaphoreType.DMA,
            pltpu.SemaphoreType.DMA((corr, 2)),
            pltpu.SemaphoreType.DMA((corr, 2)),
            pltpu.SemaphoreType.DMA((corr, count)),
            pltpu.SemaphoreType.DMA((corr, count)),
        ],
        out_shape=jax.ShapeDtypeStruct((count, corr, rows, LANES), jnp.bfloat16),
        compiler_params=pltpu.CompilerParams(
            collective_id=0, has_side_effects=True, vmem_limit_bytes=60 * 1024 * 1024
        ),
        name="regrouped_products",
    )(order, kernels, comp, taper)


def exchange_kernel(count, order_ref, finished_ref, out_ref, stage_ref, send_sem, recv_sem):
    corr = finished_ref.shape[0]
    me = lax.axis_index("facet")
    barrier = pltpu.get_barrier_semaphore()
    for off in range(1, count):
        pl.semaphore_signal(
            barrier, inc=1, device_id={"facet": lax.rem(me + off, count)}, device_id_type=MESH
        )
    for d in range(count):
        for c in range(corr):
            stage_ref[d, c] = finished_ref[c, order_ref[d]]
    pl.semaphore_wait(barrier, count - 1)
    copies = []
    for off in range(1, count):
        peer = lax.rem(me + off, count)
        copy = pltpu.make_async_remote_copy(
            src_ref=stage_ref.at[peer],
            dst_ref=out_ref.at[me],
            send_sem=send_sem.at[off],
            recv_sem=recv_sem.at[off],
            device_id={"facet": peer},
            device_id_type=MESH,
        )
        copy.start()
        copies.append(copy)
    out_ref[me] = stage_ref[me]
    for copy in copies:
        copy.wait()


def exchanged(finished, order):
    corr, count, rows, cols = finished.shape
    whole = pl.BlockSpec(memory_space=pltpu.VMEM)
    shape = (count, corr, rows, cols)
    return pl.pallas_call(
        functools.partial(exchange_kernel, count),
        in_specs=[pl.BlockSpec(memory_space=pltpu.SMEM), whole],
        out_specs=whole,
        scratch_shapes=[
            pltpu.VMEM(shape, finished.dtype),
            pltpu.SemaphoreType.DMA((count,)),
            pltpu.SemaphoreType.DMA((count,)),
        ],
        out_shape=jax.ShapeDtypeStruct(shape, finished.dtype),
        compiler_params=pltpu.CompilerParams(collective_id=1, has_side_effects=True),
        name="exchanged",
    )(order, finished)


def looked_up(row, index):
    low, high = index % LANES, index // LANES
    out = None
    for chunk in range(row.shape[1] // LANES):
        table = jnp.broadcast_to(row[:, chunk * LANES : (chunk + 1) * LANES], index.shape)
        got = jnp.take_along_axis(table, low, axis=1, mode="promise_in_bounds")
        out = got if out is None else jnp.where(high == chunk, got, out)
    return out


def gain_kernel(gains_ref, index_ref, out_ref):
    p, q = index_ref[:, 0, :], index_ref[:, 1, :]
    for c in range(gains_ref.shape[0]):
        row = gains_ref[c : c + 1, :]
        out_ref[:, c, :] = looked_up(row, p) * looked_up(row, q)


def gain_products(gains, index):
    rows = index.shape[0]
    step = min(rows, 128)
    return pl.pallas_call(
        gain_kernel,
        grid=(rows // step,),
        in_specs=[
            pl.BlockSpec(gains.shape, lambda j: (0, 0)),
            pl.BlockSpec((step,) + index.shape[1:], lambda j: (j, 0, 0)),
        ],
        out_specs=pl.BlockSpec((step, gains.shape[0], index.shape[2]), lambda j: (j, 0, 0)),
        out_shape=jax.ShapeDtypeStruct((rows, gains.shape[0], index.shape[2]), jnp.float32),
        name="gain_products",
    )(gains, index)


ALIGN = 16


def degrid_kernel(corner_ref, target_ref, mine_ref, cols_ref, rows_ref, offset_ref, subgrid_ref, out_ref, turned_ref):
    facets, corr = mine_ref.shape[0], mine_ref.shape[1]
    side = cols_ref.shape[1]
    blocks, vis = offset_ref.shape[0], offset_ref.shape[2]
    tall, wide = TILE + ALIGN, 2 * LANES
    row_mats = jnp.concatenate([rows_ref[f] for f in range(facets)], axis=1)
    across = (((1,), (1,)), ((), ()))
    for c in range(corr):
        spread = jnp.concatenate(
            [
                lax.dot_general(
                    cols_ref[f], mine_ref[f, c], across, preferred_element_type=jnp.float32
                ).astype(jnp.bfloat16)
                for f in range(facets)
            ],
            axis=1,
        )
        subgrid_ref[c] = lax.dot_general(
            row_mats, spread, across, preferred_element_type=jnp.float32
        ).astype(jnp.bfloat16)
        turned_ref[c] = lax.dot_general(
            spread, row_mats, across, preferred_element_type=jnp.float32
        ).astype(jnp.bfloat16)
    out_ref[...] = jnp.zeros_like(out_ref)
    row_places = lax.broadcasted_iota(jnp.int32, (wide, vis), 0)
    col_places = lax.broadcasted_iota(jnp.int32, (tall, vis), 0)
    factor = -0.5 / (KERNEL_WIDTH * KERNEL_WIDTH)

    def weights(places, offset):
        delta = places.astype(jnp.float32) - offset
        inside = (places >= 0) & (places < TILE)
        return jnp.where(inside, jnp.exp(factor * (delta * delta)), 0.0)

    def one_block(k, carry):
        r, q = corner_ref[k, 0], corner_ref[k, 1]
        r0 = pl.multiple_of(jnp.minimum(r // LANES * LANES, side - wide), LANES)
        q0 = pl.multiple_of(jnp.minimum(q // ALIGN * ALIGN, side - tall), ALIGN)
        offsets = offset_ref[k]
        row_weights = weights(row_places - (r - r0), offsets[0:1]).astype(jnp.bfloat16)
        col_weights = weights(col_places - (q - q0), offsets[1:2])
        tile = jnp.concatenate(
            [turned_ref[c, pl.ds(q0, tall), pl.ds(r0, wide)] for c in range(corr)], axis=0
        )
        along = jnp.dot(tile, row_weights, preferred_element_type=jnp.float32)
        values = [
            jnp.sum(along[c * tall : (c + 1) * tall] * col_weights, axis=0, keepdims=True)
            for c in range(corr)
        ]
        out_ref[target_ref[k]] = jnp.concatenate(values, axis=0).astype(out_ref.dtype)
        return carry

    lax.fori_loop(0, blocks, one_block, 0, unroll=4)


def formed_and_predicted(mine, finish_cols, finish_rows, corners, offsets, target, slots):
    corr = mine.shape[1]
    side = finish_cols.shape[1]
    vis = offsets.shape[2]
    whole = pl.BlockSpec(memory_space=pltpu.VMEM)
    scalars = pl.BlockSpec(memory_space=pltpu.SMEM)
    return pl.pallas_call(
        degrid_kernel,
        in_specs=[scalars, scalars, whole, whole, whole, whole],
        out_specs=[whole, whole],
        out_shape=[
            jax.ShapeDtypeStruct((corr, side, side), jnp.bfloat16),
            jax.ShapeDtypeStruct((slots, corr, vis), jnp.bfloat16),
        ],
        scratch_shapes=[pltpu.VMEM((corr, side, side), jnp.bfloat16)],
        compiler_params=pltpu.CompilerParams(vmem_limit_bytes=32 * 1024 * 1024),
        name="formed_and_predicted",
    )(corners, target, mine, finish_cols, finish_rows, offsets)


def inverse_of(perm):
    count = perm.shape[0]
    places = jnp.arange(count, dtype=jnp.int32)
    return jnp.sum(jnp.where(perm[None, :] == places[:, None], places[None, :], 0), axis=1)


def on_device(
    sky_components,
    scale_kernels,
    row_taper,
    col_taper,
    finish_rows,
    finish_cols,
    subgrid_owner,
    block_cell,
    vis_offset,
    block_owner,
    observed,
    antenna_pair_index,
    gains,
):
    n_facet = lax.axis_size("facet")
    n_strip = lax.axis_size("strip")
    devices = n_facet * n_strip
    comp = sky_components[0]
    corr = comp.shape[0]
    rows = comp.shape[2]
    facet_side = comp.shape[3]
    contrib_side = finish_cols.shape[2]
    sub_rows = row_taper.shape[2] // contrib_side
    sub_cols = col_taper.shape[2] // contrib_side
    col_perm = subgrid_owner[:sub_cols] % n_strip
    row_perm = subgrid_owner.reshape(sub_rows, sub_cols)[:, 0] // n_strip
    col_inverse = inverse_of(col_perm)
    row_inverse = inverse_of(row_perm)
    regrouped = regrouped_products(comp, scale_kernels, col_taper[0], col_inverse)
    all_rows = row_taper[0].reshape(n_strip, rows, sub_rows * contrib_side)
    finished = jnp.einsum(
        "xrm,xcrj->cmj", all_rows, regrouped, preferred_element_type=jnp.float32
    ).astype(jnp.bfloat16)
    mine = exchanged(finished.reshape(corr, sub_rows, contrib_side, contrib_side), row_inverse)
    blocks = block_owner.shape[0]
    visibility_block = observed.shape[2]
    dest = block_owner[:, 0]
    same = dest[:, None] == dest[None, :]
    order = jnp.arange(blocks, dtype=jnp.int32)
    earlier = order[None, :] < order[:, None]
    rank = jnp.sum((same & earlier).astype(jnp.int32), axis=1)
    capacity = observed.shape[0] // devices
    target = dest * capacity + rank
    subgrid, outgoing_vis = formed_and_predicted(
        mine, finish_cols, finish_rows, block_cell, vis_offset, target, devices * capacity
    )
    outgoing_vis = outgoing_vis.reshape(devices, capacity, corr, visibility_block)
    arrived = lax.all_to_all(
        outgoing_vis, ("facet", "strip"), split_axis=0, concat_axis=0, tiled=True
    ).astype(jnp.float32)
    placed = arrived.reshape(devices * capacity, corr, visibility_block)
    product = gain_products(gains, antenna_pair_index)
    residual = observed - product * placed
    return (subgrid[None], residual)


def solution(mesh):
    placed = (
        P("facet", None, None, "strip", None),
        P(),
        P("facet", None, None),
        P("facet", None, None),
        P(),
        P(),
        P(),
        P(("facet", "strip"), None),
        P(("facet", "strip"), None, None),
        P(("facet", "strip"), None),
        P(("facet", "strip"), None, None),
        P(("facet", "strip"), None, None),
        P(),
    )
    return jax.shard_map(
        on_device,
        mesh=mesh,
        in_specs=placed,
        out_specs=(P(("facet", "strip"), None, None, None), P(("facet", "strip"), None, None)),
        check_vma=False,
    )
```
